32 devices in a mesh: parts: 2 (over y), turn: 4 (over x, core), branch: 4 (over z).
Axes of the slice: x: 2, y: 2, z: 4, core: 2. Of those that a mesh axis runs over, the one named last changes fastest.
Arguments:
- query: bfloat16 [4096, 4096], P(('parts', 'turn', 'branch')), parts along dimension 0, may hold values from -128 to 128
- branch_key_value: bfloat16 [2, 4096, 512], P(None, ('parts', 'turn', 'branch')), parts along dimension 1, may hold values from -4 to 4
- turn_key_value: bfloat16 [2, 64, 512], P(None, ('parts', 'turn', 'branch')), parts along dimension 1, may hold values from -4 to 4
- kv_trunk: bfloat16 [2, 32, 512], P(None, ('parts', 'turn', 'branch')), parts along dimension 1, may hold values from -4 to 4
- grad_out: bfloat16 [4096, 4096], P(('parts', 'turn', 'branch')), parts along dimension 0, may hold values from -6 to 6
- branch_lengths: int32 [32, 4], P(('parts', 'turn', 'branch')), parts along dimension 0, may hold values from 1 to 64, 128 in all within a row
- parents: int32 [8], P('parts'), parts along dimension 0, may hold values from -1 to 2, as said below
Outputs:
- attended: bfloat16 [4096, 4096], P(('parts', 'turn', 'branch')), parts along dimension 0
- grad_query: bfloat16 [4096, 4096], P(('parts', 'turn', 'branch')), parts along dimension 0
- grad_branch_kv: bfloat16 [2, 4096, 512], P(None, ('parts', 'turn', 'branch')), parts along dimension 1
- grad_turn_kv: bfloat16 [2, 64, 512], P(None, ('parts', 'turn', 'branch')), parts along dimension 1
- grad_trunk_kv: bfloat16 [2, 32, 512], P(None, ('parts', 'turn', 'branch')), parts along dimension 1
The draws below stay inside these ranges and needn't reach their ends.
There are 2 independent parts, one for each index of `parts`. The reference program is written for one: setup_inputs(seed, part) draws one part's arguments, and reference() takes and returns one part's arrays. A program takes and returns all parts, laid end to end along the dimension named above; each array names one. Nothing has to cross between parts.
Inputs may be any that keep to these rules, and one draw needn't show every extreme that they name: parents[t] is -1 or a turn before t; parents[0] is -1 and the last turn's parent is the turn before it.
All inputs are finite; a program needn't handle non-finite values.
Results may differ from the reference program's by a relative error of at most 0.02.
Values may be sent and summed in bfloat16 or wider, within the bound.
No kernel may reach another device: no remote copies, remote signals or barrier semaphores. Data moves between devices by JAX's collectives and lax.ppermute only.
A program may use at most 64 MiB of HBM per device.

```python
import math
import jax
import jax.numpy as jnp
import numpy as np
from jax import lax

QUERY_HEADS = 32
KEY_VALUE_HEADS = 4
HEAD_SIZE = 128
QUERY_PER_KEY = 8
NB = 4
BRANCH_DEV = 128
MOST = 64
TURNS = 4
TRUNK_TOKENS = 16
TURN_TOKENS = 32
BRANCH_TOKENS = 2048
N_BRANCH = 4


def trunk_key_rows(key):
    base_offset = jnp.clip(jax.random.normal(jax.random.fold_in(key, 11), (TRUNK_TOKENS, KEY_VALUE_HEADS * HEAD_SIZE), jnp.float32), -4.0, 4.0)
    return base_offset


def draw_kv_trunk(key, part):
    key_part = trunk_key_rows(key)
    value_portion = jnp.clip(jax.random.normal(jax.random.fold_in(key, 13), (TRUNK_TOKENS, KEY_VALUE_HEADS * HEAD_SIZE), jnp.float32), -4.0, 4.0)
    return jnp.stack([key_part, value_portion]).astype(jnp.bfloat16)


def draw_query(key, part):
    normal_part = jax.random.normal(jax.random.fold_in(key, 21), (BRANCH_TOKENS, QUERY_HEADS * HEAD_SIZE), jnp.float32)
    return jnp.clip(normal_part, -4.0, 4.0).astype(jnp.bfloat16)


def draw_parents(key, part):
    limit = jnp.arange(TURNS, dtype=jnp.int32) + 1
    drawn = jax.random.randint(jax.random.fold_in(key, 31), (TURNS,), 0, limit, dtype=jnp.int32) - 1
    position = jnp.arange(TURNS, dtype=jnp.int32)
    return jnp.where(position == TURNS - 1, jnp.int32(TURNS - 2), drawn).astype(jnp.int32)


def steps_of(key, extent, cuts, low, high):
    level, own = 1.0, jax.random.fold_in(key, 6)
    for dim, parts in cuts:
        draws = jnp.exp(jax.random.uniform(jax.random.fold_in(own, dim), (parts,), jnp.float32, low / len(cuts), high / len(cuts)))
        level = level * jnp.repeat(draws, extent[dim] // parts).reshape([-1 if axis == dim else 1 for axis in range(len(extent))])
    return level


def length_profile(number_of, total, most, skew):
    loads = [(1 << 20) // math.isqrt(rank ** skew) + 1 for rank in range(2, number_of + 1)]
    spare, holding = total - most - (number_of - 1), [1] * (number_of - 1)
    while spare > 0:
        free = [i for i in range(number_of - 1) if holding[i] < most]
        whole, budget = sum([loads[i] for i in free]), spare
        for i in free:
            extra = min(most - holding[i], max(1, budget * loads[i] // whole), spare)
            holding[i] = holding[i] + extra
            spare = spare - extra
    return np.array([most] + holding)


def ragged(own_key, amount, total, most, skew):
    if amount == 2:
        one = jax.random.randint(own_key, (), max(1, total - most), min(most, total - 1) + 1)
        return jnp.stack([one, total - one])
    tallies = jnp.asarray(length_profile(amount, total, most, skew), jnp.int32)
    pairs = (amount - 1) // 2
    giver, taker = tallies[1:1 + 2 * pairs:2], tallies[2:2 + 2 * pairs:2]
    slack = jnp.minimum(giver - 1, most - taker)
    shifted = jax.random.randint(jax.random.fold_in(own_key, 1), (pairs,), 0, 1 << 20) % (slack + 1)
    tallies = tallies.at[1:1 + 2 * pairs:2].set(giver - shifted).at[2:2 + 2 * pairs:2].set(taker + shifted)
    return tallies[jax.random.permutation(jax.random.fold_in(own_key, 2), amount)]


def bell_draw(own_key, extent, width, bound, split=(), kind=jnp.bfloat16):
    values = width * jax.random.normal(own_key, extent, jnp.float32)
    if split:
        values = values * steps_of(own_key, extent, split, -0.22, 0.18)
    return jnp.clip(values, -bound, bound).astype(kind)


def setup_inputs(seed: int = 0, part: int = 0) -> dict:
    key_list = jax.random.split(jax.random.key(seed), 8)
    part_keys = jax.random.split(jax.random.fold_in(key_list[7], part), 8)
    query = draw_query(jax.random.fold_in(jax.random.fold_in(key_list[7], part), 71), part)
    branch_key_value = bell_draw(part_keys[1], (2, BRANCH_TOKENS, KEY_VALUE_HEADS * HEAD_SIZE), 1.0, 4.0, ((1, 16),))
    turn_key_value = bell_draw(part_keys[2], (2, TURN_TOKENS, KEY_VALUE_HEADS * HEAD_SIZE), 1.0, 4.0, ((1, 16),))
    kv_trunk = draw_kv_trunk(jax.random.fold_in(jax.random.fold_in(key_list[7], part), 71), part)
    grad_out = bell_draw(part_keys[4], (BRANCH_TOKENS, QUERY_HEADS * HEAD_SIZE), 1.0, 6.0, ((0, 16),))
    branch_lengths = jax.vmap(lambda own: ragged(own, NB, BRANCH_DEV, MOST, 2))(jax.random.split(part_keys[5], (TURNS * N_BRANCH))).reshape((TURNS * N_BRANCH, NB)).astype(jnp.int32)
    parents = draw_parents(jax.random.fold_in(jax.random.fold_in(key_list[7], part), 71), part)
    return dict(query=query, branch_key_value=branch_key_value, turn_key_value=turn_key_value, kv_trunk=kv_trunk, grad_out=grad_out, branch_lengths=branch_lengths, parents=parents)


masked_score = -1e+30

def ancestry(parents, turn_count):
    position = jnp.arange(turn_count, dtype=jnp.int32)
    parent_of = parents[:, None] == position[None, :]
    start = position[:, None] == position[None, :]

    def widen(sweep, reached):
        return reached | jnp.any(reached[:, :, None] & parent_of[None, :, :], axis=1)
    return lax.fori_loop(0, turn_count, widen, start)

def visible(path_row, lengths, trunk_rows, turn_rows, turn_count, branch_rows):
    turn_length = turn_rows // turn_count
    owner_turn = jnp.arange(turn_rows, dtype=jnp.int32) // turn_length
    on_path = jnp.any((owner_turn[:, None] == jnp.arange(turn_count, dtype=jnp.int32)[None, :]) & path_row[None, :], axis=1)
    segment_ends = jnp.cumsum(lengths, dtype=jnp.int32)
    position = jnp.arange(branch_rows, dtype=jnp.int32)
    segment = lax.optimization_barrier(jnp.sum((position[:, None] >= segment_ends[None, :]).astype(jnp.int32), axis=1))
    inside = (segment[:, None] == segment[None, :]) & (position[None, :] <= position[:, None])
    leading = jnp.ones((branch_rows, trunk_rows), dtype=bool)
    middle = jnp.broadcast_to(on_path[None, :], (branch_rows, turn_rows))
    return jnp.concatenate([leading, middle, inside], axis=1)

def group_terms(query, key_rows, values, grad_out, allowed, group_index):
    query_total = query.shape[0]
    group_width = QUERY_PER_KEY * HEAD_SIZE
    softmax_scale = 1.0 / math.sqrt(HEAD_SIZE)
    start = group_index * group_width
    queries = lax.dynamic_slice_in_dim(query, start, group_width, 1).reshape(query_total, QUERY_PER_KEY, HEAD_SIZE).astype(jnp.float32)
    cotangent = lax.dynamic_slice_in_dim(grad_out, start, group_width, 1).reshape(query_total, QUERY_PER_KEY, HEAD_SIZE).astype(jnp.float32)
    head_keys = lax.dynamic_slice_in_dim(key_rows, group_index * HEAD_SIZE, HEAD_SIZE, 1).astype(jnp.float32)
    head_values = lax.dynamic_slice_in_dim(values, group_index * HEAD_SIZE, HEAD_SIZE, 1).astype(jnp.float32)
    scores = jnp.einsum('rgd,kd->grk', queries, head_keys) * softmax_scale
    scores = jnp.where(allowed[None, :, :], scores, masked_score)
    largest = lax.optimization_barrier(jnp.max(scores, axis=2, keepdims=True))
    exponent = jnp.exp(scores - largest)
    probs = exponent / lax.optimization_barrier(jnp.sum(exponent, axis=2, keepdims=True))
    rounded = lax.optimization_barrier(probs.astype(jnp.bfloat16)).astype(jnp.float32)
    attended = jnp.einsum('grk,kd->rgd', rounded, head_values).astype(jnp.bfloat16)
    attended_wide = lax.optimization_barrier(attended).astype(jnp.float32)
    delta = lax.optimization_barrier(jnp.sum(cotangent * attended_wide, axis=2))
    dprob = jnp.einsum('rgd,kd->grk', cotangent, head_values)
    dscore = (probs * (dprob - jnp.transpose(delta)[:, :, None])).astype(jnp.bfloat16)
    dscore_wide = lax.optimization_barrier(dscore).astype(jnp.float32)
    grad_query = (jnp.einsum('grk,kd->rgd', dscore_wide, head_keys) * softmax_scale).astype(jnp.bfloat16)
    grad_keys = jnp.einsum('grk,rgd->kd', dscore_wide, queries) * softmax_scale
    grad_values = jnp.einsum('grk,rgd->kd', rounded, cotangent)
    return (attended.reshape(query_total, group_width), grad_query.reshape(query_total, group_width), grad_keys, grad_values)

def device_terms(query, key_rows, values, grad_out, allowed):
    query_total = query.shape[0]
    key_total = key_rows.shape[0]
    group_width = QUERY_PER_KEY * HEAD_SIZE

    def single_group(group_index, totals):
        attended, grad_query, grad_keys, grad_values = totals
        piece_out, piece_query, piece_keys, piece_values = group_terms(query, key_rows, values, grad_out, allowed, group_index)
        attended = lax.dynamic_update_slice_in_dim(attended, piece_out, group_index * group_width, 1)
        grad_query = lax.dynamic_update_slice_in_dim(grad_query, piece_query, group_index * group_width, 1)
        grad_keys = lax.dynamic_update_slice_in_dim(grad_keys, piece_keys, group_index * HEAD_SIZE, 1)
        grad_values = lax.dynamic_update_slice_in_dim(grad_values, piece_values, group_index * HEAD_SIZE, 1)
        return (attended, grad_query, grad_keys, grad_values)
    initial_state = (jnp.zeros((query_total, QUERY_HEADS * HEAD_SIZE), jnp.bfloat16), jnp.zeros((query_total, QUERY_HEADS * HEAD_SIZE), jnp.bfloat16), jnp.zeros((key_total, KEY_VALUE_HEADS * HEAD_SIZE), jnp.float32), jnp.zeros((key_total, KEY_VALUE_HEADS * HEAD_SIZE), jnp.float32))
    return lax.fori_loop(0, KEY_VALUE_HEADS, single_group, initial_state)

def reference(query, branch_key_value, turn_key_value, kv_trunk, grad_out, branch_lengths, parents):
    block_count = TURNS * N_BRANCH
    feature_dim = KEY_VALUE_HEADS * HEAD_SIZE
    shared_rows = TRUNK_TOKENS + TURN_TOKENS
    reached = ancestry(parents, TURNS)
    shared_keys = jnp.concatenate([kv_trunk[0], turn_key_value[0]], axis=0)
    shared_values = jnp.concatenate([kv_trunk[1], turn_key_value[1]], axis=0)
    query_blocks = query.reshape(block_count, BRANCH_DEV, QUERY_HEADS * HEAD_SIZE)
    grad_blocks = grad_out.reshape(block_count, BRANCH_DEV, QUERY_HEADS * HEAD_SIZE)
    branch_blocks = jnp.swapaxes(branch_key_value.reshape(2, block_count, BRANCH_DEV, feature_dim), 0, 1)

    def one_block(totals, pieces):
        block_index, block_query, block_kv, block_grad, lengths = pieces
        turn_index = block_index // N_BRANCH
        path_row = jnp.any(reached & (jnp.arange(TURNS, dtype=jnp.int32)[:, None] == turn_index), axis=0)
        allowed = visible(path_row, lengths, TRUNK_TOKENS, TURN_TOKENS, TURNS, BRANCH_DEV)
        key_rows = jnp.concatenate([shared_keys, block_kv[0]], axis=0)
        value_rows = jnp.concatenate([shared_values, block_kv[1]], axis=0)
        attended, grad_query, grad_keys, grad_values = device_terms(block_query, key_rows, value_rows, block_grad, allowed)
        shared = jnp.stack([grad_keys[:shared_rows], grad_values[:shared_rows]])
        own = jnp.stack([grad_keys[shared_rows:], grad_values[shared_rows:]]).astype(jnp.bfloat16)
        return (totals + shared, (attended, grad_query, own))
    start = jnp.zeros((2, shared_rows, feature_dim), jnp.float32)
    pieces = (jnp.arange(block_count, dtype=jnp.int32), query_blocks, branch_blocks, grad_blocks, branch_lengths)
    totals, outputs = lax.scan(one_block, start, pieces)
    attended = outputs[0].reshape(BRANCH_TOKENS, QUERY_HEADS * HEAD_SIZE)
    grad_query = outputs[1].reshape(BRANCH_TOKENS, QUERY_HEADS * HEAD_SIZE)
    grad_branch_kv = jnp.swapaxes(outputs[2], 0, 1).reshape(2, BRANCH_TOKENS, feature_dim)
    grad_trunk_kv = totals[:, :TRUNK_TOKENS].astype(jnp.bfloat16)
    grad_turn_kv = totals[:, TRUNK_TOKENS:].astype(jnp.bfloat16)
    return (attended, grad_query, grad_branch_kv, grad_turn_kv, grad_trunk_kv)
```

```python
import functools
import math

import jax
import jax.numpy as jnp
from jax import lax
from jax.experimental import pallas as pl
from jax.experimental.pallas import tpu as pltpu
from jax.sharding import PartitionSpec as P

HEAD_SIZE = 128
masked_score = -1e30


def exchange_steps(mesh):
    steps = []
    for axis in ("branch", "turn"):
        size = mesh.shape[axis]
        assert size & (size - 1) == 0
        bit = size // 2
        while bit:
            steps.append((axis, bit, size))
            bit //= 2
    return steps


def swap(x, axis, bit, size):
    return lax.ppermute(x, axis, [(i, i ^ bit) for i in range(size)])


def kernel(
    steps, trunk_rows, turn_rows, turns, parents_ref, lengths_ref, q_ref, kv_ref, shared_ref,
    do_ref, out_ref, dq_ref, dkv_ref, keep_ref, send_ref, bias_ref, w_ref, ds_ref,
):
    group = pl.program_id(0)
    queries = q_ref.shape[0]
    slots = shared_ref.shape[0]
    rows = trunk_rows + turn_rows
    shared = slots * rows
    features = kv_ref.shape[2] * pl.num_programs(0)
    heads = q_ref.shape[1] // HEAD_SIZE
    scale = 1.0 / math.sqrt(HEAD_SIZE)
    f32 = jnp.float32
    bf16 = jnp.bfloat16

    @pl.when(group == 0)
    def _():
        me = lax.axis_index("turn")
        slot = lax.broadcasted_iota(jnp.int32, (slots, queries), 0)
        away = jnp.zeros_like(slot)
        for k, (axis, bit, _) in enumerate(steps):
            if axis == "turn":
                away = away + ((slot >> k) & 1) * bit
        owner = jnp.bitwise_xor(away, me)
        path = owner == me
        at = me
        for _ in range(turns - 1):
            at = jnp.where(at >= 0, parents_ref[jnp.maximum(at, 0)], -1)
            path = path | (owner == at)
        turn_bias = jnp.where(path, 0.0, masked_score).astype(f32)
        for r in range(rows):
            piece = jnp.zeros_like(turn_bias) if r < trunk_rows else turn_bias
            bias_ref[r * slots:(r + 1) * slots, :] = piece
        key_at = lax.broadcasted_iota(jnp.int32, (queries, queries), 0)
        query_at = lax.broadcasted_iota(jnp.int32, (queries, queries), 1)
        first = jnp.zeros_like(query_at)
        end = jnp.int32(0)
        for c in range(lengths_ref.shape[1]):
            end = end + lengths_ref[0, c]
            first = jnp.where(query_at >= end, end, first)
        inside = (key_at >= first) & (key_at <= query_at)
        bias_ref[shared:, :] = jnp.where(inside, 0.0, masked_score).astype(f32)

    lane = pl.multiple_of(group * HEAD_SIZE, HEAD_SIZE)

    def gathered(part):
        pieces = [
            shared_ref[:, pl.ds((2 * r + part) * features + lane, HEAD_SIZE)] for r in range(rows)
        ]
        return jnp.concatenate(pieces + [kv_ref[part]], axis=0)

    keys, values = gathered(0), gathered(1)
    keys_t = keys.T
    values_t = values.T
    per = 2 if heads % 2 == 0 else 1
    bias = jnp.concatenate([bias_ref[...]] * per, axis=1)
    nt = (((1,), (1,)), ((), ()))
    nn = (((1,), (0,)), ((), ()))

    def stacked(ref, lo, hi):
        return jnp.concatenate(
            [ref[:, h * HEAD_SIZE:(h + 1) * HEAD_SIZE] for h in range(lo, hi)], axis=0
        )

    def unstack(ref, lo, value):
        turned = value.T
        for h in range(per):
            ref[:, (lo + h) * HEAD_SIZE:(lo + h + 1) * HEAD_SIZE] = turned[
                h * queries:(h + 1) * queries, :
            ]

    for lo in range(0, heads, per):
        q = stacked(q_ref, lo, lo + per)
        do = stacked(do_ref, lo, lo + per)
        s = lax.dot_general(keys, q, nt, preferred_element_type=f32) + bias
        top = jnp.max(s, axis=0, keepdims=True)
        e = jnp.exp((s - top) * scale)
        p = e * (1.0 / jnp.sum(e, axis=0, keepdims=True))
        w = p.astype(bf16)
        dp = lax.dot_general(values, do, nt, preferred_element_type=f32)
        delta = jnp.sum(p * dp, axis=0, keepdims=True)
        ds = (p * (dp - delta)).astype(bf16)
        span = slice(lo * queries, (lo + per) * queries)
        w_ref[:, span] = w
        ds_ref[:, span] = ds
        o_t = lax.dot_general(values_t, w, nn, preferred_element_type=f32)
        unstack(out_ref, lo, o_t.astype(bf16))
        dq_t = lax.dot_general(keys_t, ds, nn, preferred_element_type=f32) * scale
        unstack(dq_ref, lo, dq_t.astype(bf16))

    dk = lax.dot_general(
        ds_ref[...], stacked(q_ref, 0, heads), nn, preferred_element_type=f32
    ) * scale
    dv = lax.dot_general(w_ref[...], stacked(do_ref, 0, heads), nn, preferred_element_type=f32)
    dkv_ref[0] = dk[shared:].astype(bf16)
    dkv_ref[1] = dv[shared:].astype(bf16)
    half = slots // 2
    for part, grad in ((0, dk), (1, dv)):
        for r in range(rows):
            at_lane = pl.ds((2 * r + part) * features + lane, HEAD_SIZE)
            keep_ref[:, at_lane] = grad[r * slots:r * slots + half]
            send_ref[:, at_lane] = grad[r * slots + half:(r + 1) * slots].astype(bf16)


def on_device(mesh, query, branch_kv, turn_kv, trunk_kv, grad_out, lengths, parents):
    steps = exchange_steps(mesh)
    slots = 2 ** len(steps)
    queries, width = query.shape
    features = branch_kv.shape[2]
    groups = features // HEAD_SIZE
    trunk_rows, turn_rows = trunk_kv.shape[1], turn_kv.shape[1]
    rows = trunk_rows + turn_rows
    flat = rows * 2 * features

    own = jnp.concatenate([trunk_kv, turn_kv], axis=1)
    held = jnp.swapaxes(own, 0, 1).reshape(1, flat)
    for axis, bit, size in steps:
        held = jnp.concatenate([held, swap(held, axis, bit, size)], axis=0)

    bf16 = jnp.bfloat16
    key_rows = slots * rows + queries
    block = pl.BlockSpec((queries, width // groups), lambda g: (0, g))
    kv_block = pl.BlockSpec((2, queries, HEAD_SIZE), lambda g: (0, 0, g))
    whole = lambda n: pl.BlockSpec((n, flat), lambda g: (0, 0))
    smem = pl.BlockSpec(memory_space=pltpu.SMEM)
    attended, grad_query, grad_branch, keep, send = pl.pallas_call(
        functools.partial(kernel, steps, trunk_rows, turn_rows, mesh.shape["turn"]),
        grid=(groups,),
        in_specs=[smem, smem, block, kv_block, whole(slots), block],
        out_specs=[block, block, kv_block, whole(slots // 2), whole(slots // 2)],
        out_shape=[
            jax.ShapeDtypeStruct(query.shape, bf16),
            jax.ShapeDtypeStruct(query.shape, bf16),
            jax.ShapeDtypeStruct(branch_kv.shape, bf16),
            jax.ShapeDtypeStruct((slots // 2, flat), jnp.float32),
            jax.ShapeDtypeStruct((slots // 2, flat), bf16),
        ],
        scratch_shapes=[
            pltpu.VMEM((key_rows, queries), jnp.float32),
            pltpu.VMEM((key_rows, queries * (width // features)), bf16),
            pltpu.VMEM((key_rows, queries * (width // features)), bf16),
        ],
        name="tree_attention",
    )(parents, lengths, query, branch_kv, held, grad_out)

    total = keep
    for k in reversed(range(len(steps))):
        axis, bit, size = steps[k]
        if k < len(steps) - 1:
            half = total.shape[0] // 2
            send, total = total[half:].astype(bf16), total[:half]
        total = total + swap(send, axis, bit, size).astype(jnp.float32)
    total = jnp.swapaxes(total.astype(bf16).reshape(rows, 2, features), 0, 1)
    return attended, grad_query, grad_branch, total[:, trunk_rows:], total[:, :trunk_rows]


def solution(mesh):
    everywhere = ("parts", "turn", "branch")
    by_row = P(everywhere, None)
    by_middle = P(None, everywhere, None)
    return jax.shard_map(
        functools.partial(on_device, mesh),
        mesh=mesh,
        in_specs=(by_row, by_middle, by_middle, by_middle, by_row, by_row, P("parts")),
        out_specs=(by_row, by_row, by_middle, by_middle, by_middle),
        check_vma=False,
    )
```

```python
import functools
import math

import jax
import jax.numpy as jnp
from jax import lax
from jax.experimental import pallas as pl
from jax.experimental.pallas import tpu as pltpu
from jax.sharding import PartitionSpec as P


HEAD_SIZE = 128
masked_score = -1e30
softmax_scale = 1.0 / math.sqrt(HEAD_SIZE)
exp2_scale = softmax_scale * math.log2(math.e)
f32 = jnp.float32
bf16 = jnp.bfloat16
NT = (((1,), (1,)), ((), ()))
NN = (((1,), (0,)), ((), ()))
vmem = pl.BlockSpec(memory_space=pltpu.VMEM)
smem = pl.BlockSpec(memory_space=pltpu.SMEM)


def exchange_steps(mesh):
    steps = []
    for axis in ("branch", "turn"):
        size = mesh.shape[axis]
        assert size & (size - 1) == 0
        bit = size // 2
        while bit:
            steps.append((axis, bit, size))
            bit //= 2
    return steps


def swap(x, step):
    axis, bit, size = step
    return lax.ppermute(x, axis, [(i, i ^ bit) for i in range(size)])


def dot(a, b, dims):
    return lax.dot_general(a, b, dims, preferred_element_type=f32)


def stacked(ref, lo, hi):
    return jnp.concatenate(
        [ref[:, h * HEAD_SIZE:(h + 1) * HEAD_SIZE] for h in range(lo, hi)], axis=0
    )


def head_chunks(first, last, per_group, per):
    for group in range(first, last):
        for lo in range(group * per_group, (group + 1) * per_group, per):
            yield group, lo


def own_kernel(first_group, per_group, per, lengths_ref, q_ref, do_ref, kv_ref, e_ref, dp_ref, stat_ref):
    queries = q_ref.shape[0]
    groups = e_ref.shape[1] // (queries * per_group)
    key_at = lax.broadcasted_iota(jnp.int32, (queries, queries), 0)
    query_at = lax.broadcasted_iota(jnp.int32, (queries, queries), 1)
    start = jnp.zeros_like(query_at)
    end = jnp.int32(0)
    for c in range(lengths_ref.shape[1]):
        end = end + lengths_ref[0, c]
        start = jnp.where(query_at >= end, end, start)
    inside = (key_at >= start) & (key_at <= query_at)
    bias = jnp.where(inside, 0.0, masked_score).astype(f32)
    bias = jnp.concatenate([bias] * per, axis=1)
    base = first_group * per_group
    for group, lo in head_chunks(first_group, first_group + groups, per_group, per):
        lanes = slice(group * HEAD_SIZE, (group + 1) * HEAD_SIZE)
        span = slice((lo - base) * queries, (lo - base + per) * queries)
        s = dot(kv_ref[0, :, lanes], stacked(q_ref, lo, lo + per), NT) + bias
        top = jnp.max(s, axis=0, keepdims=True)
        e = jnp.exp2((s - top) * exp2_scale)
        dp = dot(kv_ref[1, :, lanes], stacked(do_ref, lo, lo + per), NT)
        e_ref[:, span] = e
        dp_ref[:, span] = dp
        stat_ref[0:1, span] = top
        stat_ref[1:2, span] = jnp.sum(e, axis=0, keepdims=True)
        stat_ref[2:3, span] = jnp.sum(e * dp, axis=0, keepdims=True)


def shared_rows_of(shared_ref, rows, features, part, group):
    return jnp.concatenate(
        [
            shared_ref[:, pl.ds((2 * r + part) * features + group * HEAD_SIZE, HEAD_SIZE)]
            for r in range(rows)
        ],
        axis=0,
    )


def shared_kernel(
    steps, trunk_rows, turn_rows, turns, per_group, per, parts, parents_ref, near_ref, far_ref, q_ref, do_ref, *refs
):
    stat_refs, refs = refs[:parts], refs[parts:]
    shared_ref, w_ref, ds_ref, joined_ref, keep_ref, send_ref = refs
    queries = q_ref.shape[0]
    slots = shared_ref.shape[0]
    shared_ref[:slots // 2] = near_ref[...]
    shared_ref[slots // 2:] = far_ref[...]
    rows = trunk_rows + turn_rows
    features = shared_ref.shape[1] // (2 * rows)
    groups = features // HEAD_SIZE
    half = slots // 2

    me = lax.axis_index("turn")
    slot = lax.broadcasted_iota(jnp.int32, (slots, per * queries), 0)
    away = jnp.zeros_like(slot)
    for k, (axis, bit, _) in enumerate(steps):
        if axis == "turn":
            away = away + ((slot >> k) & 1) * bit
    owner = jnp.bitwise_xor(away, me)
    path = owner == me
    at = me
    for _ in range(turns - 1):
        at = jnp.where(at >= 0, parents_ref[jnp.maximum(at, 0)], -1)
        path = path | (owner == at)
    turn_bias = jnp.where(path, 0.0, masked_score).astype(f32)
    bias = jnp.concatenate(
        [jnp.zeros_like(turn_bias)] * trunk_rows + [turn_bias] * turn_rows, axis=0
    )

    for group in range(groups):
        keys = shared_rows_of(shared_ref, rows, features, 0, group)
        values = shared_rows_of(shared_ref, rows, features, 1, group)
        first, last = group * per_group, (group + 1) * per_group
        for lo in range(first, last, per):
            span = slice(lo * queries, (lo + per) * queries)
            part, place = divmod(lo, groups * per_group // parts)
            stat_ref = stat_refs[part]
            stat = slice(place * queries, (place + per) * queries)
            own_top = stat_ref[0:1, stat]
            s = dot(keys, stacked(q_ref, lo, lo + per), NT) + bias
            top = jnp.maximum(jnp.max(s, axis=0, keepdims=True), own_top)
            e = jnp.exp2((s - top) * exp2_scale)
            shrink = jnp.exp2((own_top - top) * exp2_scale)
            dp = dot(values, stacked(do_ref, lo, lo + per), NT)
            total = jnp.sum(e, axis=0, keepdims=True) + shrink * stat_ref[1:2, stat]
            inverse = 1.0 / total
            delta = inverse * (
                jnp.sum(e * dp, axis=0, keepdims=True) + shrink * stat_ref[2:3, stat]
            )
            p = e * inverse
            w_ref[:, span] = p.astype(bf16)
            ds_ref[:, span] = (p * (dp - delta)).astype(bf16)
            joined_ref[0:1, span] = shrink * inverse
            joined_ref[1:2, span] = delta
        span = slice(first * queries, last * queries)
        dk = dot(ds_ref[:, span], stacked(q_ref, first, last), NN) * softmax_scale
        dv = dot(w_ref[:, span], stacked(do_ref, first, last), NN)
        for part, grad in ((0, dk), (1, dv)):
            for r in range(rows):
                at_lane = pl.ds((2 * r + part) * features + group * HEAD_SIZE, HEAD_SIZE)
                keep_ref[:, at_lane] = grad[r * slots:r * slots + half]
                send_ref[:, at_lane] = grad[r * slots + half:(r + 1) * slots].astype(bf16)


def back_kernel(
    group, place, rows, per_group, per, aliased, q_ref, do_ref, kv_ref, shared_ref, ws_ref, dss_ref, joined_ref,
    e_ref, dp_ref, *refs,
):
    out_ref, dq_ref, dkv_ref, w_ref, ds_ref = refs[aliased:]
    queries = q_ref.shape[0]
    features = kv_ref.shape[2]
    lanes = slice(group * HEAD_SIZE, (group + 1) * HEAD_SIZE)

    def turned(part):
        shared = shared_rows_of(shared_ref, rows, features, part, group)
        return jnp.concatenate([shared, kv_ref[part, :, lanes]], axis=0).T

    keys_t, values_t = turned(0), turned(1)

    def unstack(ref, lo, value):
        back = value.T
        for h in range(per):
            ref[:, (lo + h) * HEAD_SIZE:(lo + h + 1) * HEAD_SIZE] = back[h * queries:(h + 1) * queries]

    for lo in range(0, per_group, per):
        span = slice(lo * queries, (lo + per) * queries)
        stored = slice((place + lo) * queries, (place + lo + per) * queries)
        whole = slice((group * per_group + lo) * queries, (group * per_group + lo + per) * queries)
        p = e_ref[:, stored] * joined_ref[0:1, whole]
        w = p.astype(bf16)
        ds = (p * (dp_ref[:, stored] - joined_ref[1:2, whole])).astype(bf16)
        w_ref[:, span] = w
        ds_ref[:, span] = ds
        o_t = dot(values_t, jnp.concatenate([ws_ref[:, whole], w], axis=0), NN)
        unstack(out_ref, lo, o_t.astype(bf16))
        dq_t = dot(keys_t, jnp.concatenate([dss_ref[:, whole], ds], axis=0), NN) * softmax_scale
        unstack(dq_ref, lo, dq_t.astype(bf16))
    first, last = group * per_group, (group + 1) * per_group
    dk = dot(ds_ref[...], stacked(q_ref, first, last), NN) * softmax_scale
    dv = dot(w_ref[...], stacked(do_ref, first, last), NN)
    dkv_ref[0] = dk.astype(bf16)
    dkv_ref[1] = dv.astype(bf16)


def pack_kernel(trunk_rows, features, trunk_ref, turn_ref, out_ref):
    rows = out_ref.shape[1] // (2 * features)
    for r in range(rows):
        for part in range(2):
            lane = (2 * r + part) * features
            if r < trunk_rows:
                piece = trunk_ref[part, r:r + 1, :]
            else:
                piece = turn_ref[part, r - trunk_rows:r - trunk_rows + 1, :]
            out_ref[:, lane:lane + features] = piece


def finish_kernel(trunk_rows, features, total_ref, last_ref, trunk_ref, turn_ref):
    total = (total_ref[...] + last_ref[...].astype(f32)).astype(bf16)
    rows = total.shape[1] // (2 * features)
    for r in range(rows):
        for part in range(2):
            lane = (2 * r + part) * features
            piece = total[:, lane:lane + features]
            if r < trunk_rows:
                trunk_ref[part, r:r + 1, :] = piece
            else:
                turn_ref[part, r - trunk_rows:r - trunk_rows + 1, :] = piece


params = pltpu.CompilerParams(vmem_limit_bytes=16 * 2 ** 20)


def on_device(mesh, query, branch_kv, turn_kv, trunk_kv, grad_out, lengths, parents):
    steps = exchange_steps(mesh)
    slots = 2 ** len(steps)
    queries, width = query.shape
    features = branch_kv.shape[2]
    groups = features // HEAD_SIZE
    per_group = width // features
    per = 2 if per_group % 2 == 0 else 1
    parts = groups
    trunk_rows, turn_rows = trunk_kv.shape[1], turn_kv.shape[1]
    rows = trunk_rows + turn_rows
    flat = rows * 2 * features
    spread = queries * per_group
    shape = jax.ShapeDtypeStruct

    own_parts = []
    for part in range(parts):
        own_parts.append(pl.pallas_call(
            functools.partial(own_kernel, part * groups // parts, per_group, per),
            in_specs=[smem, vmem, vmem, vmem],
            out_specs=[vmem] * 3,
            out_shape=[
                shape((queries, spread * groups // parts), f32),
                shape((queries, spread * groups // parts), f32),
                shape((8, spread * groups // parts), f32),
            ],
            compiler_params=params,
        )(lengths, query, grad_out, branch_kv))

    near = pl.pallas_call(
        functools.partial(pack_kernel, trunk_rows, features),
        in_specs=[vmem] * 2,
        out_specs=vmem,
        out_shape=shape((1, flat), bf16),
        compiler_params=params,
        name="pack",
    )(trunk_kv, turn_kv)
    for k, step in enumerate(steps):
        if k:
            near = jnp.concatenate([near, far], axis=0)
        far = swap(near, step)

    held, shared_w, shared_ds, joined, total, send = pl.pallas_call(
        functools.partial(
            shared_kernel, steps, trunk_rows, turn_rows, mesh.shape["turn"], per_group, per, parts
        ),
        in_specs=[smem] + [vmem] * (4 + parts),
        out_specs=[vmem] * 6,
        out_shape=[
            shape((slots, flat), bf16),
            shape((slots * rows, spread * groups), bf16),
            shape((slots * rows, spread * groups), bf16),
            shape((8, spread * groups), f32),
            shape((slots // 2, flat), f32),
            shape((slots // 2, flat), bf16),
        ],
        compiler_params=params,
        name="shared",
    )(parents, near, far, query, grad_out, *[p[2] for p in own_parts])

    made = ()
    block = lambda g: pl.BlockSpec((queries, spread_width), lambda i: (0, g))
    spread_width = width // groups
    for group in range(groups):
        part, place = divmod(group, groups // parts)
        e, dp, _ = own_parts[part]
        made = pl.pallas_call(
            functools.partial(back_kernel, group, place * per_group, rows, per_group, per, len(made)),
            grid=(1,),
            in_specs=[vmem] * 9 + [pl.BlockSpec(memory_space=pl.ANY)] * len(made),
            out_specs=[
                block(group), block(group),
                pl.BlockSpec((2, queries, HEAD_SIZE), lambda i, g=group: (0, 0, g)),
            ],
            out_shape=[
                shape(query.shape, bf16), shape(query.shape, bf16), shape(branch_kv.shape, bf16)
            ],
            scratch_shapes=[pltpu.VMEM((queries, spread), bf16)] * 2,
            input_output_aliases={9 + i: i for i in range(len(made))},
            compiler_params=params,
        )(query, grad_out, branch_kv, held, shared_w, shared_ds, joined, e, dp, *made)

    for k in reversed(range(len(steps))):
        came = swap(send, steps[k])
        if k:
            total = total + came.astype(f32)
            half = total.shape[0] // 2
            send, total = total[half:].astype(bf16), total[:half]
    grad_trunk, grad_turn = pl.pallas_call(
        functools.partial(finish_kernel, trunk_rows, features),
        in_specs=[vmem] * 2,
        out_shape=[shape(trunk_kv.shape, bf16), shape(turn_kv.shape, bf16)],
        compiler_params=params,
        name="finish",
    )(total, came)
    return (*made, grad_turn, grad_trunk)


def solution(mesh):
    everywhere = ("parts", "turn", "branch")
    by_row = P(everywhere, None)
    by_middle = P(None, everywhere, None)

    def layer(*args):
        return on_device(mesh, *args)

    return jax.shard_map(
        layer,
        mesh=mesh,
        in_specs=(by_row, by_middle, by_middle, by_middle, by_row, by_row, P("parts")),
        out_specs=(by_row, by_row, by_middle, by_middle, by_middle),
        check_vma=False,
    )
```

```python
import functools
import math

import jax
import jax.numpy as jnp
from jax import lax
from jax.experimental import pallas as pl
from jax.experimental.pallas import tpu as pltpu
from jax.sharding import PartitionSpec as P


HEAD_SIZE = 128
masked_score = -1e30
softmax_scale = 1.0 / math.sqrt(HEAD_SIZE)
exp2_scale = softmax_scale * math.log2(math.e)
f32 = jnp.float32
bf16 = jnp.bfloat16
NT = (((1,), (1,)), ((), ()))
NN = (((1,), (0,)), ((), ()))
vmem = pl.BlockSpec(memory_space=pltpu.VMEM)
hbm = pl.BlockSpec(memory_space=pltpu.HBM)


def exchange_steps(mesh):
    steps = []
    for axis in ("branch", "turn"):
        size = mesh.shape[axis]
        assert size & (size - 1) == 0
        bit = size // 2
        while bit:
            steps.append((axis, bit, size))
            bit //= 2
    return steps


def swap(x, step):
    axis, bit, size = step
    return lax.ppermute(x, axis, [(i, i ^ bit) for i in range(size)])


def in_hbm(x):
    return pltpu.with_memory_space_constraint(x, pltpu.HBM)


def dot(a, b, dims):
    return lax.dot_general(a, b, dims, preferred_element_type=f32)


def load_kernel(
    steps, trunk_rows, turn_rows, turns, q_hbm, do_hbm, kv_hbm, lengths_hbm, parents_hbm,
    q_ref, do_ref, kv_ref, own_bias_ref, bias_ref, lengths_ref, parents_ref, sems,
):
    queries = q_hbm.shape[0]
    slots = 2 ** len(steps)
    small = [
        pltpu.make_async_copy(lengths_hbm, lengths_ref, sems.at[0]),
        pltpu.make_async_copy(parents_hbm, parents_ref, sems.at[1]),
    ]
    for copy in small:
        copy.start()
    for part in range(2):
        for g in range(kv_hbm.shape[2] // HEAD_SIZE):
            pltpu.make_async_copy(
                kv_hbm.at[part, :, pl.ds(g * HEAD_SIZE, HEAD_SIZE)], kv_ref.at[part, g], sems.at[2]
            ).start()
    for h in range(q_hbm.shape[1] // HEAD_SIZE):
        lanes = pl.ds(h * HEAD_SIZE, HEAD_SIZE)
        place = pl.ds(h * queries, queries)
        pltpu.make_async_copy(q_hbm.at[:, lanes], q_ref.at[place], sems.at[3]).start()
        pltpu.make_async_copy(do_hbm.at[:, lanes], do_ref.at[place], sems.at[4]).start()
    for copy in small:
        copy.wait()

    key_at = lax.broadcasted_iota(jnp.int32, (queries, queries), 0)
    query_at = lax.broadcasted_iota(jnp.int32, (queries, queries), 1)
    start = jnp.zeros_like(query_at)
    end = jnp.int32(0)
    for c in range(lengths_ref.shape[1]):
        end = end + lengths_ref[0, c]
        start = jnp.where(query_at >= end, end, start)
    inside = (key_at >= start) & (key_at <= query_at)
    own_bias_ref[...] = jnp.where(inside, 0.0, masked_score).astype(f32)

    me = lax.axis_index("turn")
    slot = lax.broadcasted_iota(jnp.int32, (slots, queries), 0)
    away = jnp.zeros_like(slot)
    for k, (axis, bit, _) in enumerate(steps):
        if axis == "turn":
            away = away + ((slot >> k) & 1) * bit
    owner = jnp.bitwise_xor(away, me)
    path = owner == me
    at = me
    for _ in range(turns - 1):
        at = jnp.where(at >= 0, parents_ref[jnp.maximum(at, 0)], -1)
        path = path | (owner == at)
    turn_bias = jnp.where(path, 0.0, masked_score).astype(f32)
    for r in range(trunk_rows + turn_rows):
        piece = jnp.zeros_like(turn_bias) if r < trunk_rows else turn_bias
        bias_ref[r * slots:(r + 1) * slots] = piece

    for ref, sem in ((kv_ref, 2), (q_ref, 3), (do_ref, 4)):
        pltpu.make_async_copy(ref, ref, sems.at[sem]).wait()


def head_chunks(first, last, per_group, per):
    for group in range(first, last):
        for lo in range(group * per_group, (group + 1) * per_group, per):
            yield group, lo


def own_kernel(first_group, per_group, per, q_ref, do_ref, kv_ref, bias_ref, e_ref, dp_ref, stat_ref):
    queries = bias_ref.shape[0]
    groups = e_ref.shape[1] // (queries * per_group)
    bias = jnp.concatenate([bias_ref[...]] * per, axis=1)
    base = first_group * per_group
    for group, lo in head_chunks(first_group, first_group + groups, per_group, per):
        heads = slice(lo * queries, (lo + per) * queries)
        span = slice((lo - base) * queries, (lo - base + per) * queries)
        s = dot(kv_ref[0, group], q_ref[heads], NT) + bias
        top = jnp.max(s, axis=0, keepdims=True)
        e = jnp.exp2((s - top) * exp2_scale)
        dp = dot(kv_ref[1, group], do_ref[heads], NT)
        e_ref[:, span] = e
        dp_ref[:, span] = dp
        stat_ref[0:1, span] = top
        stat_ref[1:2, span] = jnp.sum(e, axis=0, keepdims=True)
        stat_ref[2:3, span] = jnp.sum(e * dp, axis=0, keepdims=True)


def shared_rows_of(shared_ref, rows, features, part, group):
    return jnp.concatenate(
        [
            shared_ref[:, pl.ds((2 * r + part) * features + group * HEAD_SIZE, HEAD_SIZE)]
            for r in range(rows)
        ],
        axis=0,
    )


def shared_kernel(
    trunk_rows, turn_rows, per_group, per, parts, near_ref, far_ref, q_ref, do_ref, bias_ref, *refs
):
    stat_refs, refs = refs[:parts], refs[parts:]
    shared_ref, w_ref, ds_ref, joined_ref, keep_ref, send_ref = refs
    queries = bias_ref.shape[1]
    slots = shared_ref.shape[0]
    shared_ref[:slots // 2] = near_ref[...]
    shared_ref[slots // 2:] = far_ref[...]
    rows = trunk_rows + turn_rows
    features = shared_ref.shape[1] // (2 * rows)
    groups = features // HEAD_SIZE
    half = slots // 2
    shared = rows * slots
    bias = jnp.concatenate([bias_ref[...]] * per, axis=1)

    for group in range(groups):
        keys = shared_rows_of(shared_ref, rows, features, 0, group)
        values = shared_rows_of(shared_ref, rows, features, 1, group)
        first, last = group * per_group, (group + 1) * per_group
        all_w, all_ds = [], []
        for lo in range(first, last, per):
            heads = slice(lo * queries, (lo + per) * queries)
            part, place = divmod(lo, groups * per_group // parts)
            stat_ref = stat_refs[part]
            stat = slice(place * queries, (place + per) * queries)
            own_top = stat_ref[0:1, stat]
            s = dot(keys, q_ref[heads], NT) + bias
            top = jnp.maximum(jnp.max(s, axis=0, keepdims=True), own_top)
            e = jnp.exp2((s - top) * exp2_scale)
            shrink = jnp.exp2((own_top - top) * exp2_scale)
            dp = dot(values, do_ref[heads], NT)
            total = jnp.sum(e, axis=0, keepdims=True) + shrink * stat_ref[1:2, stat]
            inverse = 1.0 / total
            delta = inverse * (
                jnp.sum(e * dp, axis=0, keepdims=True) + shrink * stat_ref[2:3, stat]
            )
            p = e * inverse
            w = p.astype(bf16)
            ds = (p * (dp - delta)).astype(bf16)
            for h in range(per):
                place = slice((lo + h) * shared, (lo + h + 1) * shared)
                w_ref[place] = w[:, h * queries:(h + 1) * queries]
                ds_ref[place] = ds[:, h * queries:(h + 1) * queries]
            all_w.append(w)
            all_ds.append(ds)
            joined_ref[0:1, heads] = shrink * inverse
            joined_ref[1:2, heads] = delta
        heads = slice(first * queries, last * queries)
        dk = dot(jnp.concatenate(all_ds, axis=1), q_ref[heads], NN) * softmax_scale
        dv = dot(jnp.concatenate(all_w, axis=1), do_ref[heads], NN)
        for part, grad in ((0, dk), (1, dv)):
            for r in range(rows):
                at_lane = pl.ds((2 * r + part) * features + group * HEAD_SIZE, HEAD_SIZE)
                keep_ref[:, at_lane] = grad[r * slots:r * slots + half]
                send_ref[:, at_lane] = grad[r * slots + half:(r + 1) * slots].astype(bf16)


def back_kernel(
    group, place, rows, per_group, per, aliased, q_ref, do_ref, kv_ref, shared_ref, ws_ref, dss_ref, joined_ref,
    e_ref, dp_ref, *refs,
):
    out_ref, dq_ref, dkv_ref, w_ref, ds_ref = refs[aliased:]
    queries = kv_ref.shape[2]
    features = kv_ref.shape[1] * HEAD_SIZE
    shared = shared_ref.shape[0] * rows

    def turned(part):
        before = shared_rows_of(shared_ref, rows, features, part, group)
        return jnp.concatenate([before, kv_ref[part, group]], axis=0).T

    keys_t, values_t = turned(0), turned(1)

    def all_rows(ref, head, own):
        before = [ref[(head + h) * shared:(head + h + 1) * shared] for h in range(per)]
        return jnp.concatenate([jnp.concatenate(before, axis=1), own], axis=0)

    def unstack(ref, lo, value):
        back = value.T
        for h in range(per):
            ref[:, (lo + h) * HEAD_SIZE:(lo + h + 1) * HEAD_SIZE] = back[h * queries:(h + 1) * queries]

    for lo in range(0, per_group, per):
        head = group * per_group + lo
        span = slice(lo * queries, (lo + per) * queries)
        stored = slice((place + lo) * queries, (place + lo + per) * queries)
        whole = slice(head * queries, (head + per) * queries)
        p = e_ref[:, stored] * joined_ref[0:1, whole]
        w = p.astype(bf16)
        ds = (p * (dp_ref[:, stored] - joined_ref[1:2, whole])).astype(bf16)
        w_ref[:, span] = w
        ds_ref[:, span] = ds
        o_t = dot(values_t, all_rows(ws_ref, head, w), NN)
        unstack(out_ref, lo, o_t.astype(bf16))
        dq_t = dot(keys_t, all_rows(dss_ref, head, ds), NN) * softmax_scale
        unstack(dq_ref, lo, dq_t.astype(bf16))
    heads = slice(group * per_group * queries, (group + 1) * per_group * queries)
    dk = dot(ds_ref[...], q_ref[heads], NN) * softmax_scale
    dv = dot(w_ref[...], do_ref[heads], NN)
    dkv_ref[0] = dk.astype(bf16)
    dkv_ref[1] = dv.astype(bf16)


def pack_kernel(trunk_rows, features, trunk_hbm, turn_hbm, out_ref, trunk_ref, turn_ref, sems):
    copies = [
        pltpu.make_async_copy(trunk_hbm, trunk_ref, sems.at[0]),
        pltpu.make_async_copy(turn_hbm, turn_ref, sems.at[1]),
    ]
    for copy in copies:
        copy.start()
    for copy in copies:
        copy.wait()
    rows = out_ref.shape[1] // (2 * features)
    for r in range(rows):
        for part in range(2):
            lane = (2 * r + part) * features
            if r < trunk_rows:
                piece = trunk_ref[r, part:part + 1, :]
            else:
                piece = turn_ref[part, r - trunk_rows:r - trunk_rows + 1, :]
            out_ref[:, lane:lane + features] = piece


def finish_kernel(trunk_rows, features, total_ref, last_ref, trunk_ref, turn_ref):
    total = (total_ref[...] + last_ref[...].astype(f32)).astype(bf16)
    rows = total.shape[1] // (2 * features)
    for r in range(rows):
        for part in range(2):
            lane = (2 * r + part) * features
            piece = total[:, lane:lane + features]
            if r < trunk_rows:
                trunk_ref[r, part:part + 1, :] = piece
            else:
                turn_ref[part, r - trunk_rows:r - trunk_rows + 1, :] = piece


params = pltpu.CompilerParams(vmem_limit_bytes=16 * 2 ** 20)


def on_device(mesh, query, branch_kv, turn_kv, trunk_kv, grad_out, lengths, parents):
    steps = exchange_steps(mesh)
    slots = 2 ** len(steps)
    queries, width = query.shape
    features = branch_kv.shape[2]
    groups = features // HEAD_SIZE
    per_group = width // features
    per = 2 if per_group % 2 == 0 else 1
    parts = 2 if groups % 2 == 0 else 1
    trunk_rows, turn_rows = trunk_kv.shape[1], turn_kv.shape[1]
    rows = trunk_rows + turn_rows
    flat = rows * 2 * features
    spread = queries * per_group
    shape = jax.ShapeDtypeStruct

    heads = groups * per_group
    q, do, kv, own_bias, bias = pl.pallas_call(
        functools.partial(load_kernel, steps, trunk_rows, turn_rows, mesh.shape["turn"]),
        in_specs=[hbm] * 5,
        out_specs=[vmem] * 5,
        out_shape=[
            shape((heads * queries, HEAD_SIZE), bf16),
            shape((heads * queries, HEAD_SIZE), bf16),
            shape((2, groups, queries, HEAD_SIZE), bf16),
            shape((queries, queries), f32),
            shape((slots * rows, queries), f32),
        ],
        scratch_shapes=[
            pltpu.SMEM(lengths.shape, jnp.int32),
            pltpu.SMEM(parents.shape, jnp.int32),
            pltpu.SemaphoreType.DMA((5,)),
        ],
        compiler_params=params,
        name="load",
    )(*[in_hbm(x) for x in (query, grad_out, branch_kv, lengths, parents)])

    own_parts = []
    for part in range(parts):
        own_parts.append(pl.pallas_call(
            functools.partial(own_kernel, part * groups // parts, per_group, per),
            in_specs=[vmem] * 4,
            out_specs=[vmem] * 3,
            out_shape=[
                shape((queries, spread * groups // parts), f32),
                shape((queries, spread * groups // parts), f32),
                shape((8, spread * groups // parts), f32),
            ],
            compiler_params=params,
        )(q, do, kv, own_bias))

    near = pl.pallas_call(
        functools.partial(pack_kernel, trunk_rows, features),
        in_specs=[hbm] * 2,
        out_specs=vmem,
        out_shape=shape((1, flat), bf16),
        scratch_shapes=[
            pltpu.VMEM((trunk_rows, 2, features), bf16),
            pltpu.VMEM(turn_kv.shape, bf16),
            pltpu.SemaphoreType.DMA((2,)),
        ],
        compiler_params=params,
        name="pack",
    )(in_hbm(jnp.swapaxes(trunk_kv, 0, 1)), in_hbm(turn_kv))
    for k, step in enumerate(steps):
        if k:
            near = jnp.concatenate([near, far], axis=0)
        far = swap(near, step)

    held, shared_w, shared_ds, joined, total, send = pl.pallas_call(
        functools.partial(shared_kernel, trunk_rows, turn_rows, per_group, per, parts),
        in_specs=[vmem] * (5 + parts),
        out_specs=[vmem] * 6,
        out_shape=[
            shape((slots, flat), bf16),
            shape((heads * slots * rows, queries), bf16),
            shape((heads * slots * rows, queries), bf16),
            shape((8, spread * groups), f32),
            shape((slots // 2, flat), f32),
            shape((slots // 2, flat), bf16),
        ],
        compiler_params=params,
        name="shared",
    )(near, far, q, do, bias, *[p[2] for p in own_parts])

    made = ()
    block = lambda g: pl.BlockSpec((queries, spread_width), lambda i: (0, g))
    spread_width = width // groups
    for group in range(groups):
        part, place = divmod(group, groups // parts)
        e, dp, _ = own_parts[part]
        made = pl.pallas_call(
            functools.partial(back_kernel, group, place * per_group, rows, per_group, per, len(made)),
            grid=(1,),
            in_specs=[vmem] * 9 + [hbm] * len(made),
            out_specs=[
                block(group), block(group),
                pl.BlockSpec((2, queries, HEAD_SIZE), lambda i, g=group: (0, 0, g)),
            ],
            out_shape=[
                shape(query.shape, bf16), shape(query.shape, bf16), shape(branch_kv.shape, bf16)
            ],
            scratch_shapes=[pltpu.VMEM((queries, spread), bf16)] * 2,
            input_output_aliases={9 + i: i for i in range(len(made))},
            compiler_params=params,
        )(q, do, kv, held, shared_w, shared_ds, joined, e, dp, *made)

    for k in reversed(range(len(steps))):
        came = swap(send, steps[k])
        if k:
            total = total + came.astype(f32)
            half = total.shape[0] // 2
            send, total = total[half:].astype(bf16), total[:half]
    grad_trunk, grad_turn = pl.pallas_call(
        functools.partial(finish_kernel, trunk_rows, features),
        in_specs=[vmem] * 2,
        out_shape=[shape((trunk_rows, 2, features), bf16), shape(turn_kv.shape, bf16)],
        compiler_params=params,
        name="finish",
    )(total, came)
    return (*made, grad_turn, jnp.swapaxes(grad_trunk, 0, 1))


def solution(mesh):
    everywhere = ("parts", "turn", "branch")
    by_row = P(everywhere, None)
    by_middle = P(None, everywhere, None)

    def layer(*args):
        return on_device(mesh, *args)

    return jax.shard_map(
        layer,
        mesh=mesh,
        in_specs=(by_row, by_middle, by_middle, by_middle, by_row, by_row, P("parts")),
        out_specs=(by_row, by_row, by_middle, by_middle, by_middle),
        check_vma=False,
    )
```
